512 devices in a mesh: gx: 4 (over x), gy: 16 (over z, core), gz: 8 (over y).
Axes of the slice: x: 4, y: 8, z: 8, core: 2. Of those that a mesh axis runs over, the one named last changes fastest.
Arguments:
- sketch: float32 [8, 32, 16, 64, 384], P('gx', 'gy', 'gz'), may hold values from -1200 to 1200
- test_matrix: bfloat16 [8, 32, 16, 64, 384], P('gx', 'gy', 'gz'), may hold values from -0.1796875 to 0.1796875
- offsets: bfloat16 [8, 32, 16, 3, 128], P('gx', 'gy', 'gz'), may hold values from 0 to 1
- near: int32 [8, 32, 16, 27], P('gx', 'gy', 'gz'), may hold values 0 or 1
Outputs:
- leaf_basis: float32 [8, 32, 16, 64, 384], P('gx', 'gy', 'gz')
- level1_transfer: float32 [4, 16, 8, 64, 512], P('gx', 'gy', 'gz')
- level2_basis: float32 [8, 32, 16, 64, 384], P('gx', 'gy', 'gz')
The draws below stay inside these ranges and needn't reach their ends.
All inputs are finite; a program needn't handle non-finite values. No bound on the sum of `near` on one device may be relied on, other than what follows from the above.
Results may differ from the reference program's by a relative error of at most 0.0029.
Values may be sent and summed in bfloat16 or wider, within the bound.
A program may use at most 64 MiB of HBM per device.

```python
import math
import jax
import jax.numpy as jnp
from jax import lax

NODES = 128
RANK = 64
LEAF_ROWS = 384
LEAVES_X = 8
LEAVES_Y = 32
LEAVES_Z = 16
N_GX = 4
N_GY = 16
N_GZ = 8


def draw_sketch(key, part):
    key_sign = jax.random.fold_in(key, 11)
    key_size = jax.random.fold_in(key, 12)
    key_common = jax.random.fold_in(key, 13)
    key_noise = jax.random.fold_in(key, 14)
    whole_shape = (LEAVES_X, LEAVES_Y, LEAVES_Z, RANK, LEAF_ROWS)
    signs = (2 * jax.random.randint(key_sign, (RANK,), 0, 2) - 1).astype(jnp.float32)
    sizes = jax.random.uniform(key_size, (RANK,), jnp.float32, 0.5, 1.5)
    amplitude = 160.0
    noise = 2.0 * jax.random.truncated_normal(key_noise, -4.0, 4.0, whole_shape, jnp.float32)
    common = jax.random.truncated_normal(key_common, -4.0, 4.0, (LEAVES_X, LEAVES_Y, LEAVES_Z, 1, LEAF_ROWS), jnp.float32)
    coupling = (amplitude * signs * sizes)[:, None]
    return (coupling * common + noise).astype(jnp.float32)


def touch_ends(values, rng, low, largest):
    spot = [jax.random.randint(jax.random.fold_in(rng, axis), (), 0, length) for axis, length in enumerate(values.shape)]
    main_axis = values.shape.index(max(values.shape))
    neighbour = spot[:main_axis] + [(spot[main_axis] + 1) % values.shape[main_axis]] + spot[main_axis + 1:]
    return values.at[tuple(spot)].set(low).at[tuple(neighbour)].set(largest)


def levels(rng, dims, pieces, low, largest):
    def one(position, parts):
        steps = jax.random.uniform(jax.random.fold_in(jax.random.fold_in(rng, 6), position), (parts,), jnp.float32, low / len(pieces), largest / len(pieces))
        return jnp.repeat(jnp.exp(steps), dims[position] // parts).reshape((-1,) + (1,) * (len(dims) - position - 1))

    level = one(*pieces[0])
    for cut in pieces[1:]:
        level = level * one(*cut)
    return level


def gaussian(own_key, dims, scale, most, pieces=(), kind=jnp.bfloat16):
    drawn = jax.random.normal(own_key, dims, jnp.float32) * scale
    if len(pieces) > 0:
        drawn = levels(own_key, dims, pieces, -0.22, 0.18) * drawn
    return jnp.clip(drawn, min=-most, max=most).astype(kind)


def setup_inputs(seed: int = 0) -> dict:
    streams_of = jax.random.split(jax.random.key(seed), 5)
    sketch = draw_sketch(jax.random.fold_in(streams_of[4], 71), 0)
    test_matrix = gaussian(streams_of[1], (LEAVES_X, LEAVES_Y, LEAVES_Z, RANK, LEAF_ROWS), 0.03, 0.1796875, ((0, 4), (1, 16), (2, 8)))
    offsets = jnp.clip(1.0 * jax.random.uniform(streams_of[2], (LEAVES_X, LEAVES_Y, LEAVES_Z, 3, NODES), jnp.float32) ** levels(streams_of[2], (LEAVES_X, LEAVES_Y, LEAVES_Z, 3, NODES), ((0, 4), (1, 16), (2, 8)), -0.2, 0.2), 0.0, 1.0).astype(jnp.bfloat16)
    near = touch_ends((jax.random.randint(streams_of[3], (LEAVES_X, LEAVES_Y, LEAVES_Z, 27), 0, 4) < 3).astype(jnp.int32), jax.random.fold_in(streams_of[3], 1), 0, 1)
    return {"sketch": sketch, "test_matrix": test_matrix, "offsets": offsets, "near": near}


EPSILON = 0.1
HIGHEST = lax.Precision.HIGHEST

def orthonormal(rows_t):
    gram_matrix = jnp.einsum('...km,...lm->...kl', rows_t, rows_t, precision=HIGHEST)
    first_factor = jnp.linalg.cholesky(gram_matrix)
    orthogonal = lax.linalg.triangular_solve(first_factor, rows_t, left_side=True, lower=True)
    gram_matrix = jnp.einsum('...km,...lm->...kl', orthogonal, orthogonal, precision=HIGHEST)
    second = jnp.linalg.cholesky(gram_matrix)
    orthogonal = lax.linalg.triangular_solve(second, orthogonal, left_side=True, lower=True)
    return (orthogonal, jnp.matmul(first_factor, second, precision=HIGHEST))

def shift_table():
    offset_index = jnp.arange(27, dtype=jnp.int32)
    offset_steps = jnp.stack([offset_index // 9, offset_index // 3 % 3, offset_index % 3], axis=1)
    return (1 - offset_steps).astype(jnp.float32)

def kernel_tiles(own_offsets, near_offsets, shifts):
    separation = shifts[None, :, :, None, None] + own_offsets[:, None, :, :, None] - near_offsets[:, :, :, None, :]
    square = lax.optimization_barrier(jnp.sum(separation * separation, axis=2))
    softened = square + EPSILON * EPSILON
    inverse = 1.0 / (softened * jnp.sqrt(softened))
    diagonal = (square + 2.0 * EPSILON * EPSILON) * inverse
    identity = jnp.eye(3, dtype=jnp.float32)
    kernel_block = separation[:, :, :, None] * separation[:, :, None, :] * inverse[:, :, None, None] + identity[None, None, :, :, None, None] * diagonal[:, :, None, None]
    return kernel_block.astype(jnp.bfloat16)

def reference(sketch, test_matrix, offsets, near):
    leaf_rows = 3 * NODES
    padded_test = jnp.pad(test_matrix.reshape(LEAVES_X, LEAVES_Y, LEAVES_Z, RANK, 3, NODES), ((1, 1), (1, 1), (1, 1), (0, 0), (0, 0), (0, 0)))
    float_offsets = offsets.astype(jnp.float32)
    padded_offsets = jnp.pad(float_offsets, ((1, 1), (1, 1), (1, 1), (0, 0), (0, 0)))
    shifts = shift_table()

    def column_far(column_index):
        column_x = column_index // LEAVES_Y
        column_y = column_index % LEAVES_Y
        zero = jnp.zeros((), jnp.int32)
        test_block = lax.dynamic_slice(padded_test, (column_x, column_y, zero, zero, zero, zero), (3, 3, LEAVES_Z + 2, RANK, 3, NODES))
        offset_block = lax.dynamic_slice(padded_offsets, (column_x, column_y, zero, zero, zero), (3, 3, LEAVES_Z + 2, 3, NODES))
        sampled = jnp.stack([test_block[offset_index // 9, offset_index // 3 % 3, offset_index % 3:offset_index % 3 + LEAVES_Z] for offset_index in range(27)], axis=1)
        near_offsets = jnp.stack([offset_block[offset_index // 9, offset_index // 3 % 3, offset_index % 3:offset_index % 3 + LEAVES_Z] for offset_index in range(27)], axis=1)
        near_mask = lax.dynamic_slice(near, (column_x, column_y, zero, zero), (1, 1, LEAVES_Z, 27))[0, 0]
        own_offsets = lax.dynamic_slice(float_offsets, (column_x, column_y, zero, zero, zero), (1, 1, LEAVES_Z, 3, NODES))[0, 0]
        sampled = sampled * near_mask.astype(jnp.bfloat16)[:, :, None, None, None]
        kernel_block = kernel_tiles(own_offsets, near_offsets, shifts)
        correction = jnp.einsum('bkpqij,bkcqj->bcpi', kernel_block.astype(jnp.float32), sampled.astype(jnp.float32), precision=HIGHEST)
        own_sketch = lax.dynamic_slice(sketch, (column_x, column_y, zero, zero, zero), (1, 1, LEAVES_Z, RANK, leaf_rows))[0, 0]
        return own_sketch - correction.reshape(LEAVES_Z, RANK, leaf_rows)
    far_field = lax.map(column_far, jnp.arange(LEAVES_X * LEAVES_Y, dtype=jnp.int32))
    far_field = far_field.reshape(LEAVES_X, LEAVES_Y, LEAVES_Z, RANK, leaf_rows)
    leaf_t, leaf_lower = orthonormal(far_field)
    level_in = leaf_lower.reshape(N_GX, 2, N_GY, 2, N_GZ, 2, RANK, RANK).transpose(0, 2, 4, 6, 1, 3, 5, 7).reshape(N_GX, N_GY, N_GZ, RANK, 8 * RANK)
    level_t, level_lower = orthonormal(level_in)
    top_in = level_lower.reshape(N_GX // 2, 2, N_GY // 2, 2, N_GZ // 2, 2, RANK, RANK).transpose(0, 2, 4, 6, 1, 3, 5, 7).reshape(N_GX // 2, N_GY // 2, N_GZ // 2, RANK, 8 * RANK)
    top_t, top_lower = orthonormal(top_in)
    top_blocks = top_t.reshape(N_GX // 2, N_GY // 2, N_GZ // 2, RANK, 2, 2, 2, RANK).transpose(0, 4, 1, 5, 2, 6, 3, 7).reshape(N_GX, N_GY, N_GZ, RANK, RANK)
    level_blocks = level_t.reshape(N_GX, N_GY, N_GZ, RANK, 2, 2, 2, RANK).transpose(0, 4, 1, 5, 2, 6, 3, 7).reshape(LEAVES_X, LEAVES_Y, LEAVES_Z, RANK, RANK)
    top_leaf = jnp.broadcast_to(top_blocks[:, None, :, None, :, None], (N_GX, 2, N_GY, 2, N_GZ, 2, RANK, RANK)).reshape(LEAVES_X, LEAVES_Y, LEAVES_Z, RANK, RANK)
    mixing = jnp.matmul(top_leaf, level_blocks, precision=HIGHEST)
    level2_basis = jnp.matmul(mixing, leaf_t, precision=HIGHEST) * (8.0 * math.sqrt(leaf_rows))
    leaf_basis = leaf_t * math.sqrt(leaf_rows)
    level1_transfer = level_t * math.sqrt(8 * RANK)
    return (leaf_basis, level1_transfer, level2_basis)
```

```python
import functools
import math

import jax
import jax.numpy as jnp
from jax import lax
from jax.experimental import pallas as pl
from jax.experimental.pallas import tpu as pltpu
from jax.sharding import PartitionSpec as P

EPS2 = 0.1 * 0.1
HIGHEST = lax.Precision.HIGHEST
MESH = pl.DeviceIdType.MESH
NODES = 128
F32 = jnp.float32
BF16 = jnp.bfloat16
UNROLL = 8
RANK = 64
BLOCK = 8


def directions():
    out = []
    for dx in (-1, 0, 1):
        for dy in (-1, 0, 1):
            for dz in (-1, 0, 1):
                if (dx, dy, dz) != (0, 0, 0):
                    out.append((dx, dy, dz))
    return out


def source_window(d):
    return [pl.ds(0, 2) if s == 0 else pl.ds((s + 1) // 2, 1) for s in d]


def landing_window(d):
    return [pl.ds(1, 2) if s == 0 else pl.ds(0 if s == 1 else 3, 1) for s in d]


def tile(a_rows, spread, out):
    for j in range(0, NODES, 16):
        r = [a_rows[p] - spread[p, j : j + 16, :] for p in range(3)]
        square = r[0] * r[0] + r[1] * r[1] + r[2] * r[2]
        root = lax.rsqrt(square + EPS2)
        h = root * root * root
        diagonal = (square + 2.0 * EPS2) * h
        scaled = [r[p] * h for p in range(3)]
        for p in range(3):
            for q in range(p, 3):
                block = scaled[p] * r[q]
                if p == q:
                    block = block + diagonal
                block = block.astype(BF16)
                out[q * NODES + j : q * NODES + j + 16, p * NODES : (p + 1) * NODES] = block
                if p != q:
                    out[p * NODES + j : p * NODES + j + 16, q * NODES : (q + 1) * NODES] = block


def place(kind, c, leaf, t):
    bits = [leaf // 4, leaf // 2 % 2, leaf % 2]
    first, third = (2 - c) // 2, c // 2
    marks = [first, 1 - first - third, third]
    if kind == 0:
        return [bit + 1 for bit in bits], [t // 4, t // 2 % 2, t % 2]
    if kind == 1:
        high, low = t // 2, t % 2
        b = [m * 3 * bit + (1 - m) * (bit + 1) for m, bit in zip(marks, bits)]
        a = [
            marks[0] * bits[0] + (1 - marks[0]) * high,
            marks[1] * bits[1] + marks[0] * high + marks[2] * low,
            marks[2] * bits[2] + (1 - marks[2]) * low,
        ]
        return b, a
    if kind == 2:
        b = [(1 - m) * 3 * bit + m * (bit + 1) for m, bit in zip(marks, bits)]
        a = [m * t + (1 - m) * bit for m, bit in zip(marks, bits)]
        return b, a
    return [3 * bit for bit in bits], bits


def pair_class(kind, c, near_ref, ext, ext_off, acc, spreads, tiles):
    count = 8 // 2**kind
    per = min(count, UNROLL)
    pick = (
        lax.broadcasted_iota(jnp.int32, (3, 3 * NODES), 1) // NODES
        == lax.broadcasted_iota(jnp.int32, (3, 3 * NODES), 0)
    ).astype(BF16)

    def step(n, carry):
        u = 0
        for m in range(UNROLL // per):
            first = n * UNROLL + m * per
            leaf = first // count
            b, _ = place(kind, c, leaf, 0)
            spread = lax.dot_general(
                ext_off[b[0], b[1], b[2]],
                pick,
                (((0,), (0,)), ((), ())),
                preferred_element_type=F32,
            )
            for p in range(3):
                spreads[m, p] = spread[:, p * NODES : (p + 1) * NODES]
            for k in range(per):
                b, a = place(kind, c, leaf, first % count + k)
                d = [b[k] - 1 - a[k] for k in range(3)]
                own = ext_off[a[0] + 1, a[1] + 1, a[2] + 1].astype(F32)
                rows = [own[p : p + 1, :] - d[p].astype(F32) for p in range(3)]
                tile(rows, spreads.at[m], tiles.at[u])
                index = 9 * (d[0] + 1) + 3 * (d[1] + 1) + d[2] + 1
                mask = near_ref[a[0], a[1], a[2], index].astype(F32)
                sampled = ext[b[0], b[1], b[2]] * mask.astype(BF16)
                acc[a[0], a[1], a[2]] -= jnp.dot(
                    sampled, tiles[u], preferred_element_type=F32
                )
                u += 1
        return carry

    lax.fori_loop(0, 8 * count // UNROLL, step, 0)


def all_pairs(arrive, *refs):
    arrive(0, 0)
    pair_class(0, 0, *refs)
    for kind in (1, 2):

        def step(c, carry):
            arrive(kind, c)
            pair_class(kind, c, *refs)
            return carry

        lax.fori_loop(0, 3, step, 0)
    arrive(3, 0)
    pair_class(3, 0, *refs)


def kind_of(d):
    size = sum(abs(s) for s in d)
    if size == 3:
        return 3, 0
    return size, [abs(s) for s in d].index(1 if size == 1 else 0)


def near_kernel(
    sizes, near_ref, sketch, test, offs, far, ext, ext_off, spreads, tiles, sends, recvs, o_sends, o_recvs
):
    names = ("gx", "gy", "gz")
    me = [lax.axis_index(n) for n in names]

    def inside(d):
        ok = None
        for k in range(3):
            if d[k] != 0:
                here = (me[k] < sizes[k] - 1) if d[k] == 1 else (me[k] > 0)
                ok = here if ok is None else jnp.logical_and(ok, here)
        return ok

    def copies(d):
        n = directions().index(d)
        to = tuple(me[k] + d[k] for k in range(3))
        s, t = source_window(d), landing_window(d)
        return (
            pltpu.make_async_remote_copy(
                src_ref=offs.at[s[0], s[1], s[2]],
                dst_ref=ext_off.at[t[0], t[1], t[2]],
                send_sem=o_sends.at[n],
                recv_sem=o_recvs.at[n],
                device_id=to,
                device_id_type=MESH,
            ),
            pltpu.make_async_remote_copy(
                src_ref=test.at[s[0], s[1], s[2]],
                dst_ref=ext.at[t[0], t[1], t[2]],
                send_sem=sends.at[n],
                recv_sem=recvs.at[n],
                device_id=to,
                device_id_type=MESH,
            ),
        )

    barrier = pltpu.get_barrier_semaphore()
    for d in directions():

        @pl.when(inside(d))
        def _():
            to = tuple(me[k] + d[k] for k in range(3))
            pl.semaphore_signal(barrier, inc=1, device_id=to, device_id_type=MESH)

    spans = [
        1 + (me[k] > 0).astype(jnp.int32) + (me[k] < sizes[k] - 1).astype(jnp.int32)
        for k in range(3)
    ]
    for k in range(3):
        for side in (0, 1):
            at = [slice(None)] * 3
            at[k] = slice(3 * side, 3 * side + 1)

            @pl.when(me[k] == side * (sizes[k] - 1))
            def _():
                ext[at[0], at[1], at[2]] = jnp.zeros_like(ext[at[0], at[1], at[2]])
                ext_off[at[0], at[1], at[2]] = jnp.zeros_like(ext_off[at[0], at[1], at[2]])

    pl.semaphore_wait(barrier, spans[0] * spans[1] * spans[2] - 1)
    order = sorted(directions(), key=kind_of)
    for d in order:

        @pl.when(inside(d))
        def _():
            for c in copies(d):
                c.start()

    ext[1:3, 1:3, 1:3] = test[...]
    ext_off[1:3, 1:3, 1:3] = offs[...]
    far[...] = sketch[...]

    def arrive(kind, c):
        for d in order:
            if kind_of(d)[0] == kind:

                @pl.when(jnp.logical_and(c == kind_of(d)[1], inside([-s for s in d])))
                def _():
                    for copy in copies(d):
                        copy.wait_recv()

    all_pairs(arrive, near_ref, ext, ext_off, far, spreads, tiles)
    for d in order:

        @pl.when(inside(d))
        def _():
            for c in copies(d):
                c.wait_send()


def near_field(mesh, sketch, test, offs, near):
    sizes = tuple(mesh.shape[n] for n in ("gx", "gy", "gz"))
    vmem = pl.BlockSpec(memory_space=pltpu.VMEM)
    return pl.pallas_call(
        functools.partial(near_kernel, sizes),
        out_shape=jax.ShapeDtypeStruct(sketch.shape, F32),
        in_specs=[pl.BlockSpec(memory_space=pltpu.SMEM), vmem, vmem, vmem],
        out_specs=vmem,
        scratch_shapes=[
            pltpu.VMEM((4, 4, 4) + test.shape[3:], BF16),
            pltpu.VMEM((4, 4, 4) + offs.shape[3:], BF16),
            pltpu.VMEM((UNROLL, 3, NODES, NODES), F32),
            pltpu.VMEM((UNROLL, 3 * NODES, 3 * NODES), BF16),
            pltpu.SemaphoreType.DMA((26,)),
            pltpu.SemaphoreType.DMA((26,)),
            pltpu.SemaphoreType.DMA((26,)),
            pltpu.SemaphoreType.DMA((26,)),
        ],
        compiler_params=pltpu.CompilerParams(
            collective_id=0, has_side_effects=True, vmem_limit_bytes=48 << 20
        ),
    )(near, sketch, test, offs)


def gram(rows, stage):
    stage[RANK:, :] = rows
    return lax.dot_general(
        rows,
        stage[...],
        (((1,), (1,)), ((), ())),
        precision=HIGHEST,
        preferred_element_type=F32,
    )


def product(left, right):
    return jnp.dot(left, right, precision=HIGHEST, preferred_element_type=F32)


def put(state, slot, matrix):
    eye = (
        lax.broadcasted_iota(jnp.int32, (RANK, 2 * RANK), 0)
        == lax.broadcasted_iota(jnp.int32, (RANK, 2 * RANK), 1)
    ).astype(F32)
    state[pl.ds(slot, RANK, stride=8), :] = matrix + eye


def inverse_of(state, slot):
    return state[pl.ds(slot, RANK, stride=8), :][:, :RANK]


def splat(row, lane):
    return jnp.broadcast_to(row[:, RANK + lane : RANK + lane + 1], row.shape)


def factor(states):
    for start in range(0, RANK, BLOCK):
        for state in states:
            rows = [state[8 * (start + k) : 8 * (start + k) + 8, :] for k in range(BLOCK)]
            c = {
                (k, m): splat(rows[k], start + m)
                for k in range(BLOCK)
                for m in range(k, BLOCK)
            }
            for k in range(BLOCK):
                inverse = lax.rsqrt(c[k, k])
                f = {m: c[k, m] * inverse for m in range(k + 1, BLOCK)}
                for m in range(k + 1, BLOCK):
                    for n in range(m, BLOCK):
                        c[m, n] = c[m, n] - f[m] * f[n]
                rows[k] = rows[k] * inverse
                for m in range(k + 1, BLOCK):
                    rows[m] = rows[m] - f[m] * rows[k]
                state[8 * (start + k) : 8 * (start + k) + 8, :] = rows[k]
            for i in range(start + BLOCK, RANK):
                row = state[8 * i : 8 * i + 8, :]
                for k in range(BLOCK):
                    row = row - splat(rows[k], i) * rows[k]
                state[8 * i : 8 * i + 8, :] = row


def leaves():
    return [(i, j, k) for i in range(2) for j in range(2) for k in range(2)]


def gram_kernel(far, grams, box, stage):
    stage[:RANK, :] = jnp.zeros((RANK, stage.shape[1]), F32)
    total = None
    for n, a in enumerate(leaves()):
        g = gram(far[a], stage)
        grams[n] = g
        total = g if total is None else total + g
    box[...] = total


def first_kernel(far, grams, box, group, q1, w, v, grams2, box2, group2, leaf_state, top_state, stage):
    stage[:RANK, :] = jnp.zeros((RANK, stage.shape[1]), F32)
    for n in range(8):
        put(leaf_state, n, grams[n])
    put(top_state, 0, box[...])
    for n in range(1, 8):
        put(top_state, n, group[...])
    factor([leaf_state, top_state])
    box_inverse = inverse_of(top_state, 0)
    group_inverse = inverse_of(top_state, 1)
    box_total = group_total = None
    for n, a in enumerate(leaves()):
        rows = far[a]
        x = product(inverse_of(leaf_state, n), rows)
        q1[n] = x
        grams2[n] = gram(x, stage)
        x = product(box_inverse, rows)
        w[n] = x
        g = gram(x, stage)
        box_total = g if box_total is None else box_total + g
        x = product(group_inverse, rows)
        v[n] = x
        g = gram(x, stage)
        group_total = g if group_total is None else group_total + g
    box2[...] = box_total
    group2[...] = group_total


def second_kernel(q1, w, v, grams2, box2, group2, leaf_out, level_out, nested_out, leaf_state, top_state, stage):
    for n in range(8):
        put(leaf_state, n, grams2[n])
    put(top_state, 0, box2[...])
    for n in range(1, 8):
        put(top_state, n, group2[...])
    factor([leaf_state, top_state])
    width = q1.shape[2]
    box_inverse = inverse_of(top_state, 0) * math.sqrt(8 * RANK)
    group_inverse = inverse_of(top_state, 1) * (8.0 * math.sqrt(width))
    for pair in range(4):
        block = None
        for half in range(2):
            n = 2 * pair + half
            a = leaves()[n]
            x = product(inverse_of(leaf_state, n), q1[n])
            leaf_out[a] = x * math.sqrt(width)
            nested_out[a] = product(group_inverse, v[n])
            stage[half * RANK : (half + 1) * RANK, :] = x
            stage[(1 - half) * RANK : (2 - half) * RANK, :] = jnp.zeros((RANK, width), F32)
            part = lax.dot_general(
                product(box_inverse, w[n]),
                stage[...],
                (((1,), (1,)), ((), ())),
                precision=HIGHEST,
                preferred_element_type=F32,
            )
            block = part if block is None else block + part
        level_out[0, 0, 0, :, 2 * RANK * pair : 2 * RANK * (pair + 1)] = block


def exchange_kernel(own, total, slots, sends, recvs):
    names = ("gx", "gy", "gz")
    me = [lax.axis_index(n) for n in names]
    bits = [m % 2 for m in me]
    place = (bits[0] * 2 + bits[1]) * 2 + bits[2]
    others = []
    for n in range(1, 8):
        flip = (n // 4, n // 2 % 2, n % 2)
        others.append(tuple(me[k] + flip[k] * (1 - 2 * bits[k]) for k in range(3)))
    barrier = pltpu.get_barrier_semaphore()
    for to in others:
        pl.semaphore_signal(barrier, inc=1, device_id=to, device_id_type=MESH)
    pl.semaphore_wait(barrier, 7)
    copies = [
        pltpu.make_async_remote_copy(
            src_ref=own,
            dst_ref=slots.at[place],
            send_sem=sends.at[n],
            recv_sem=recvs.at[n],
            device_id=to,
            device_id_type=MESH,
        )
        for n, to in enumerate(others)
    ]
    for c in copies:
        c.start()
    slots[place] = own[...]
    for c in copies:
        c.wait_recv()
    value = slots[0]
    for n in range(1, 8):
        value = value + slots[n]
    total[...] = value
    for c in copies:
        c.wait_send()


VMEM = pl.BlockSpec(memory_space=pltpu.VMEM)


def group_sum(own, number):
    return pl.pallas_call(
        exchange_kernel,
        out_shape=jax.ShapeDtypeStruct(own.shape, F32),
        in_specs=[VMEM],
        out_specs=VMEM,
        scratch_shapes=[
            pltpu.VMEM((8,) + own.shape, F32),
            pltpu.SemaphoreType.DMA((7,)),
            pltpu.SemaphoreType.DMA((7,)),
        ],
        compiler_params=pltpu.CompilerParams(collective_id=number, has_side_effects=True),
    )(own)


def local(kernel, outs, scratch, *args):
    return pl.pallas_call(
        kernel,
        out_shape=[jax.ShapeDtypeStruct(s, F32) for s in outs],
        in_specs=[VMEM] * len(args),
        out_specs=[VMEM] * len(outs),
        scratch_shapes=[pltpu.VMEM(s, F32) for s in scratch],
        compiler_params=pltpu.CompilerParams(vmem_limit_bytes=48 << 20),
    )(*args)


def finish(far, reduce_group):
    width = far.shape[4]
    square, slab = (RANK, 2 * RANK), (8, RANK, width)
    stage, state = (2 * RANK, width), (8 * RANK, 2 * RANK)
    grams, box = local(gram_kernel, [(8,) + square, square], [stage], far)
    group = reduce_group(box, 1)
    q1, w, v, grams2, box2, group2 = local(
        first_kernel,
        [slab, slab, slab, (8,) + square, square, square],
        [state, state, stage],
        far,
        grams,
        box,
        group,
    )
    group2 = reduce_group(group2, 2)
    return local(
        second_kernel,
        [far.shape, (1, 1, 1, RANK, 8 * RANK), far.shape],
        [state, state, stage],
        q1,
        w,
        v,
        grams2,
        box2,
        group2,
    )


def solution(mesh):
    placed = (
        P("gx", "gy", "gz", None, None),
        P("gx", "gy", "gz", None, None),
        P("gx", "gy", "gz", None, None),
        P("gx", "gy", "gz", None),
    )

    def body(sketch, test_matrix, offsets, near):
        far = near_field(mesh, sketch, test_matrix, offsets, near)
        return tuple(finish(far, group_sum))

    return jax.shard_map(
        body,
        mesh=mesh,
        in_specs=placed,
        out_specs=placed[:3],
        check_vma=False,
    )
```

```python
import functools
import math

import jax
import jax.numpy as jnp
from jax import lax
from jax.experimental import pallas as pl
from jax.experimental.pallas import tpu as pltpu
from jax.sharding import PartitionSpec as P

EPS2 = 0.1 * 0.1
HIGHEST = lax.Precision.HIGHEST
MESH = pl.DeviceIdType.MESH
NODES = 128
F32 = jnp.float32
BF16 = jnp.bfloat16
UNROLL = 8
RANK = 64
BLOCK = 8


def directions():
    out = []
    for dx in (-1, 0, 1):
        for dy in (-1, 0, 1):
            for dz in (-1, 0, 1):
                if (dx, dy, dz) != (0, 0, 0):
                    out.append((dx, dy, dz))
    return out


def source_window(d):
    return [pl.ds(0, 2) if s == 0 else pl.ds((s + 1) // 2, 1) for s in d]


def landing_window(d):
    return [pl.ds(1, 2) if s == 0 else pl.ds(0 if s == 1 else 3, 1) for s in d]


def tile(a_rows, spread, out):
    for j in range(0, NODES, 16):
        r = [a_rows[p] - spread[p, j : j + 16, :] for p in range(3)]
        square = r[0] * r[0] + r[1] * r[1] + r[2] * r[2]
        root = lax.rsqrt(square + EPS2)
        h = root * root * root
        diagonal = (square + 2.0 * EPS2) * h
        scaled = [r[p] * h for p in range(3)]
        for p in range(3):
            for q in range(p, 3):
                block = scaled[p] * r[q]
                if p == q:
                    block = block + diagonal
                block = block.astype(BF16)
                out[q * NODES + j : q * NODES + j + 16, p * NODES : (p + 1) * NODES] = block
                if p != q:
                    out[p * NODES + j : p * NODES + j + 16, q * NODES : (q + 1) * NODES] = block


def place(kind, c, leaf, t):
    bits = [leaf // 4, leaf // 2 % 2, leaf % 2]
    first, third = (2 - c) // 2, c // 2
    marks = [first, 1 - first - third, third]
    if kind == 0:
        return [bit + 1 for bit in bits], [t // 4, t // 2 % 2, t % 2]
    if kind == 1:
        high, low = t // 2, t % 2
        b = [m * 3 * bit + (1 - m) * (bit + 1) for m, bit in zip(marks, bits)]
        a = [
            marks[0] * bits[0] + (1 - marks[0]) * high,
            marks[1] * bits[1] + marks[0] * high + marks[2] * low,
            marks[2] * bits[2] + (1 - marks[2]) * low,
        ]
        return b, a
    if kind == 2:
        b = [(1 - m) * 3 * bit + m * (bit + 1) for m, bit in zip(marks, bits)]
        a = [m * t + (1 - m) * bit for m, bit in zip(marks, bits)]
        return b, a
    return [3 * bit for bit in bits], bits


def pair_class(kind, c, near_ref, ext, ext_off, acc, pick, rows8, spreads, tiles):
    count = 8 // 2**kind
    for leaf in range(8):
        b, _ = place(kind, c, leaf, 0)
        rows8[8 * leaf : 8 * leaf + 3, :] = ext_off[b[0], b[1], b[2]].astype(F32)
    spread = lax.dot_general(
        rows8[...].astype(BF16),
        pick[...],
        (((0,), (0,)), ((), ())),
        preferred_element_type=F32,
    )
    for n in range(24):
        spreads[n // 3, n % 3] = spread[:, n * NODES : (n + 1) * NODES]

    def step(n, carry):
        for u in range(UNROLL):
            leaf = (n * UNROLL + u) // count
            b, a = place(kind, c, leaf, (n * UNROLL + u) % count)
            d = [b[k] - 1 - a[k] for k in range(3)]
            own = ext_off[a[0] + 1, a[1] + 1, a[2] + 1].astype(F32)
            rows = [own[p : p + 1, :] - d[p].astype(F32) for p in range(3)]
            tile(rows, spreads.at[leaf], tiles.at[u])
            index = 9 * (d[0] + 1) + 3 * (d[1] + 1) + d[2] + 1
            mask = near_ref[a[0], a[1], a[2], index].astype(F32)
            sampled = ext[b[0], b[1], b[2]] * mask.astype(BF16)
            acc[a[0], a[1], a[2]] -= jnp.dot(
                sampled, tiles[u], preferred_element_type=F32
            )
        return carry

    lax.fori_loop(0, 8 * count // UNROLL, step, 0)


def prepare(pick, rows8):
    row = lax.broadcasted_iota(jnp.int32, pick.shape, 0)
    lane = lax.broadcasted_iota(jnp.int32, pick.shape, 1)
    wanted = jnp.logical_and(row % 8 < 3, row // 8 * 3 + row % 8 == lane // NODES)
    pick[...] = wanted.astype(F32).astype(BF16)
    rows8[...] = jnp.zeros_like(rows8)


def all_pairs(arrive, *refs):
    arrive(0, 0)
    pair_class(0, 0, *refs)
    for kind in (1, 2):

        def step(c, carry):
            arrive(kind, c)
            pair_class(kind, c, *refs)
            return carry

        lax.fori_loop(0, 3, step, 0)
    arrive(3, 0)
    pair_class(3, 0, *refs)


def kind_of(d):
    size = sum(abs(s) for s in d)
    if size == 3:
        return 3, 0
    return size, [abs(s) for s in d].index(1 if size == 1 else 0)


def near_kernel(
    sizes,
    near_ref,
    sketch,
    test,
    offs,
    far,
    grams,
    box,
    group,
    ext,
    ext_off,
    pick,
    rows8,
    spreads,
    tiles,
    stage,
    slots,
    sends,
    recvs,
    o_sends,
    o_recvs,
    g_sends,
    g_recvs,
):
    names = ("gx", "gy", "gz")
    me = [lax.axis_index(n) for n in names]

    def inside(d):
        ok = None
        for k in range(3):
            if d[k] != 0:
                here = (me[k] < sizes[k] - 1) if d[k] == 1 else (me[k] > 0)
                ok = here if ok is None else jnp.logical_and(ok, here)
        return ok

    def copies(d):
        n = directions().index(d)
        to = tuple(me[k] + d[k] for k in range(3))
        s, t = source_window(d), landing_window(d)
        return (
            pltpu.make_async_remote_copy(
                src_ref=offs.at[s[0], s[1], s[2]],
                dst_ref=ext_off.at[t[0], t[1], t[2]],
                send_sem=o_sends.at[n],
                recv_sem=o_recvs.at[n],
                device_id=to,
                device_id_type=MESH,
            ),
            pltpu.make_async_remote_copy(
                src_ref=test.at[s[0], s[1], s[2]],
                dst_ref=ext.at[t[0], t[1], t[2]],
                send_sem=sends.at[n],
                recv_sem=recvs.at[n],
                device_id=to,
                device_id_type=MESH,
            ),
        )

    barrier = pltpu.get_barrier_semaphore()
    for d in directions():

        @pl.when(inside(d))
        def _():
            to = tuple(me[k] + d[k] for k in range(3))
            pl.semaphore_signal(barrier, inc=1, device_id=to, device_id_type=MESH)

    spans = [
        1 + (me[k] > 0).astype(jnp.int32) + (me[k] < sizes[k] - 1).astype(jnp.int32)
        for k in range(3)
    ]
    for k in range(3):
        for side in (0, 1):
            at = [slice(None)] * 3
            at[k] = slice(3 * side, 3 * side + 1)

            @pl.when(me[k] == side * (sizes[k] - 1))
            def _():
                ext[at[0], at[1], at[2]] = jnp.zeros_like(ext[at[0], at[1], at[2]])
                ext_off[at[0], at[1], at[2]] = jnp.zeros_like(ext_off[at[0], at[1], at[2]])

    pl.semaphore_wait(barrier, spans[0] * spans[1] * spans[2] - 1)
    order = sorted(directions(), key=kind_of)
    for d in order:

        @pl.when(inside(d))
        def _():
            for c in copies(d):
                c.start()

    prepare(pick, rows8)
    ext[1:3, 1:3, 1:3] = test[...]
    ext_off[1:3, 1:3, 1:3] = offs[...]
    far[...] = sketch[...]

    def arrive(kind, c):
        for d in order:
            if kind_of(d)[0] == kind:

                @pl.when(jnp.logical_and(c == kind_of(d)[1], inside([-s for s in d])))
                def _():
                    for copy in copies(d):
                        copy.wait_recv()

    all_pairs(arrive, near_ref, ext, ext_off, far, pick, rows8, spreads, tiles)
    leaf_grams(far, grams, box, stage)
    swaps = group_copies(me, box, slots, g_sends, g_recvs)
    for c in swaps:
        c.start()
    collect(me, swaps, box, slots, group)
    for d in order:

        @pl.when(inside(d))
        def _():
            for c in copies(d):
                c.wait_send()


def near_field(mesh, sketch, test, offs, near):
    sizes = tuple(mesh.shape[n] for n in ("gx", "gy", "gz"))
    vmem = pl.BlockSpec(memory_space=pltpu.VMEM)
    return pl.pallas_call(
        functools.partial(near_kernel, sizes),
        out_shape=[
            jax.ShapeDtypeStruct(s, F32)
            for s in (sketch.shape, (8, RANK, 2 * RANK), (RANK, 2 * RANK), (RANK, 2 * RANK))
        ],
        in_specs=[pl.BlockSpec(memory_space=pltpu.SMEM), vmem, vmem, vmem],
        out_specs=[vmem] * 4,
        scratch_shapes=[
            pltpu.VMEM((4, 4, 4) + test.shape[3:], BF16),
            pltpu.VMEM((4, 4, 4) + offs.shape[3:], BF16),
            pltpu.VMEM((64, 24 * NODES), BF16),
            pltpu.VMEM((64, NODES), F32),
            pltpu.VMEM((8, 3, NODES, NODES), F32),
            pltpu.VMEM((UNROLL, 3 * NODES, 3 * NODES), BF16),
            pltpu.VMEM((2 * RANK, 3 * NODES), F32),
            pltpu.VMEM((8, RANK, 2 * RANK), F32),
            pltpu.SemaphoreType.DMA((26,)),
            pltpu.SemaphoreType.DMA((26,)),
            pltpu.SemaphoreType.DMA((26,)),
            pltpu.SemaphoreType.DMA((26,)),
            pltpu.SemaphoreType.DMA((7,)),
            pltpu.SemaphoreType.DMA((7,)),
        ],
        compiler_params=pltpu.CompilerParams(
            collective_id=0, has_side_effects=True, vmem_limit_bytes=48 << 20
        ),
    )(near, sketch, test, offs)


def gram(rows, stage):
    stage[RANK:, :] = rows
    return lax.dot_general(
        rows,
        stage[...],
        (((1,), (1,)), ((), ())),
        precision=HIGHEST,
        preferred_element_type=F32,
    )


def product(left, right):
    return jnp.dot(left, right, precision=HIGHEST, preferred_element_type=F32)


def gram_near_identity(rows):
    high = rows.astype(BF16)
    low = (rows - high.astype(F32)).astype(BF16)
    both = jnp.concatenate([high, low], axis=0)
    parts = lax.dot_general(
        both, both, (((1,), (1,)), ((), ())), preferred_element_type=F32
    )
    half = parts[:RANK] + parts[RANK:]
    return half + pltpu.roll(half, RANK, axis=1)


def with_eye(matrix):
    row = lax.broadcasted_iota(jnp.int32, (RANK, 2 * RANK), 0)
    lane = lax.broadcasted_iota(jnp.int32, (RANK, 2 * RANK), 1)
    return jnp.where(lane < RANK, (row == lane).astype(F32), matrix)


def put(state, slot, matrix):
    state[pl.ds(slot, RANK, stride=8), :] = with_eye(matrix)


def inverse_of(state, slot):
    return state[pl.ds(slot, RANK, stride=8), :][:, :RANK]


def splat(row, lane):
    return jnp.broadcast_to(row[:, RANK + lane : RANK + lane + 1], row.shape)


def factor(states):
    for start in range(0, RANK, BLOCK):
        for state in states:
            rows = [state[8 * (start + k) : 8 * (start + k) + 8, :] for k in range(BLOCK)]
            c = {
                (k, m): splat(rows[k], start + m)
                for k in range(BLOCK)
                for m in range(k, BLOCK)
            }
            for k in range(BLOCK):
                inverse = lax.rsqrt(c[k, k])
                f = {m: c[k, m] * inverse for m in range(k + 1, BLOCK)}
                for m in range(k + 1, BLOCK):
                    for n in range(m, BLOCK):
                        c[m, n] = c[m, n] - f[m] * f[n]
                rows[k] = rows[k] * inverse
                for m in range(k + 1, BLOCK):
                    rows[m] = rows[m] - f[m] * rows[k]
                state[8 * (start + k) : 8 * (start + k) + 8, :] = rows[k]
            for i in range(start + BLOCK, RANK):
                row = state[8 * i : 8 * i + 8, :]
                for k in range(BLOCK):
                    row = row - splat(rows[k], i) * rows[k]
                state[8 * i : 8 * i + 8, :] = row


def leaves():
    return [(i, j, k) for i in range(2) for j in range(2) for k in range(2)]


def leaf_grams(far, grams, box, stage):
    stage[:RANK, :] = jnp.zeros((RANK, stage.shape[1]), F32)
    total = None
    for n, a in enumerate(leaves()):
        g = gram(far[a], stage)
        grams[n] = g
        total = g if total is None else total + g
    box[...] = total


def first_kernel(grams, box, group, leaf_state, top_state):
    for n in range(8):
        put(leaf_state, n, grams[n])
    put(top_state, 0, box[...])
    for n in range(1, 8):
        put(top_state, n, group[...])
    factor([leaf_state, top_state])


def apply_kernel(
    far, leaf_state, top_state, q1, w, v, grams2, box2, group2, own2, slots, sends, recvs
):
    me = [lax.axis_index(n) for n in ("gx", "gy", "gz")]
    barrier = pltpu.get_barrier_semaphore()
    for to in partners(me)[1]:
        pl.semaphore_signal(barrier, inc=1, device_id=to, device_id_type=MESH)
    group_inverse = inverse_of(top_state, 1)
    total = None
    for n, a in enumerate(leaves()):
        x = product(group_inverse, far[a])
        v[n] = x
        g = gram_near_identity(x)
        total = g if total is None else total + g
    own2[...] = total
    pl.semaphore_wait(barrier, 7)
    copies = group_copies(me, own2, slots, sends, recvs)
    for c in copies:
        c.start()
    box_inverse = inverse_of(top_state, 0)
    total = None
    for n, a in enumerate(leaves()):
        both = jnp.concatenate([inverse_of(leaf_state, n), box_inverse], axis=0)
        x = product(both, far[a])
        q1[n] = x[:RANK]
        w[n] = x[RANK:]
        grams2[n] = gram_near_identity(x[:RANK])
        g = gram_near_identity(x[RANK:])
        total = g if total is None else total + g
    box2[...] = total
    collect(me, copies, own2, slots, group2)


def second_kernel(q1, w, v, grams2, box2, group2, leaf_out, level_out, nested_out, leaf_state, top_state, stage):
    for n in range(8):
        put(leaf_state, n, grams2[n])
    put(top_state, 0, box2[...])
    for n in range(1, 8):
        put(top_state, n, group2[...])
    factor([leaf_state, top_state])
    width = q1.shape[2]
    box_inverse = inverse_of(top_state, 0) * math.sqrt(8 * RANK)
    group_inverse = inverse_of(top_state, 1) * (8.0 * math.sqrt(width))
    for pair in range(4):
        block = None
        for half in range(2):
            n = 2 * pair + half
            a = leaves()[n]
            x = product(inverse_of(leaf_state, n), q1[n])
            leaf_out[a] = x * math.sqrt(width)
            nested_out[a] = product(group_inverse, v[n])
            stage[half * RANK : (half + 1) * RANK, :] = x
            stage[(1 - half) * RANK : (2 - half) * RANK, :] = jnp.zeros((RANK, width), F32)
            part = lax.dot_general(
                product(box_inverse, w[n]),
                stage[...],
                (((1,), (1,)), ((), ())),
                precision=HIGHEST,
                preferred_element_type=F32,
            )
            block = part if block is None else block + part
        level_out[0, 0, 0, :, 2 * RANK * pair : 2 * RANK * (pair + 1)] = block


def partners(me):
    bits = [m % 2 for m in me]
    others = []
    for n in range(1, 8):
        flip = (n // 4, n // 2 % 2, n % 2)
        others.append(tuple(me[k] + flip[k] * (1 - 2 * bits[k]) for k in range(3)))
    return (bits[0] * 2 + bits[1]) * 2 + bits[2], others


def group_copies(me, own, slots, sends, recvs):
    here, others = partners(me)
    return [
        pltpu.make_async_remote_copy(
            src_ref=own,
            dst_ref=slots.at[here],
            send_sem=sends.at[n],
            recv_sem=recvs.at[n],
            device_id=to,
            device_id_type=MESH,
        )
        for n, to in enumerate(others)
    ]


def collect(me, copies, own, slots, total):
    slots[partners(me)[0]] = own[...]
    for c in copies:
        c.wait_recv()
    value = slots[0]
    for n in range(1, 8):
        value = value + slots[n]
    total[...] = value
    for c in copies:
        c.wait_send()


VMEM = pl.BlockSpec(memory_space=pltpu.VMEM)


def local(kernel, outs, scratch, *args):
    return pl.pallas_call(
        kernel,
        out_shape=[jax.ShapeDtypeStruct(s, F32) for s in outs],
        in_specs=[VMEM] * len(args),
        out_specs=[VMEM] * len(outs),
        scratch_shapes=[pltpu.VMEM(s, F32) for s in scratch],
        compiler_params=pltpu.CompilerParams(vmem_limit_bytes=48 << 20),
    )(*args)


def finish(far, grams, box, group):
    width = far.shape[4]
    square, slab = (RANK, 2 * RANK), (8, RANK, width)
    stage, state = (2 * RANK, width), (8 * RANK, 2 * RANK)
    states = local(first_kernel, [state, state], [], grams, box, group)
    outs = [slab, slab, slab, (8,) + square, square, square]
    applied = pl.pallas_call(
        apply_kernel,
        out_shape=[jax.ShapeDtypeStruct(s, F32) for s in outs],
        in_specs=[VMEM] * 3,
        out_specs=[VMEM] * 6,
        scratch_shapes=[
            pltpu.VMEM(square, F32),
            pltpu.VMEM((8,) + square, F32),
            pltpu.SemaphoreType.DMA((7,)),
            pltpu.SemaphoreType.DMA((7,)),
        ],
        compiler_params=pltpu.CompilerParams(
            collective_id=1, has_side_effects=True, vmem_limit_bytes=48 << 20
        ),
    )(far, *states)
    return local(
        second_kernel,
        [far.shape, (1, 1, 1, RANK, 8 * RANK), far.shape],
        [state, state, stage],
        *applied,
    )


def solution(mesh):
    placed = (
        P("gx", "gy", "gz", None, None),
        P("gx", "gy", "gz", None, None),
        P("gx", "gy", "gz", None, None),
        P("gx", "gy", "gz", None),
    )

    def body(sketch, test_matrix, offsets, near):
        near_results = near_field(mesh, sketch, test_matrix, offsets, near)
        return tuple(finish(*near_results))

    return jax.shard_map(
        body,
        mesh=mesh,
        in_specs=placed,
        out_specs=placed[:3],
        check_vma=False,
    )
```

```python
import functools
import math

import jax
import jax.numpy as jnp
from jax import lax
from jax.experimental import pallas as pl
from jax.experimental.pallas import tpu as pltpu
from jax.sharding import PartitionSpec as P

EPS2 = 0.1 * 0.1
HIGHEST = lax.Precision.HIGHEST
MESH = pl.DeviceIdType.MESH
NODES = 128
F32 = jnp.float32
BF16 = jnp.bfloat16
UNROLL = 8
RANK = 64
BLOCK = 8


def directions():
    out = []
    for dx in (-1, 0, 1):
        for dy in (-1, 0, 1):
            for dz in (-1, 0, 1):
                if (dx, dy, dz) != (0, 0, 0):
                    out.append((dx, dy, dz))
    return out


def source_window(d):
    return [pl.ds(0, 2) if s == 0 else pl.ds((s + 1) // 2, 1) for s in d]


def landing_window(d):
    return [pl.ds(1, 2) if s == 0 else pl.ds(0 if s == 1 else 3, 1) for s in d]


def tile(a_rows, spread, out):
    for j in range(0, NODES, 16):
        r = [a_rows[p] - spread[p, j : j + 16, :] for p in range(3)]
        square = r[0] * r[0] + r[1] * r[1] + r[2] * r[2]
        root = lax.rsqrt(square + EPS2)
        h = root * root * root
        diagonal = (square + 2.0 * EPS2) * h
        scaled = [r[p] * h for p in range(3)]
        for p in range(3):
            for q in range(p, 3):
                block = scaled[p] * r[q]
                if p == q:
                    block = block + diagonal
                block = block.astype(BF16)
                out[q * NODES + j : q * NODES + j + 16, p * NODES : (p + 1) * NODES] = block
                if p != q:
                    out[p * NODES + j : p * NODES + j + 16, q * NODES : (q + 1) * NODES] = block


def place(kind, c, leaf, t):
    bits = [leaf // 4, leaf // 2 % 2, leaf % 2]
    first, third = (2 - c) // 2, c // 2
    marks = [first, 1 - first - third, third]
    if kind == 0:
        return [bit + 1 for bit in bits], [t // 4, t // 2 % 2, t % 2]
    if kind == 1:
        high, low = t // 2, t % 2
        b = [m * 3 * bit + (1 - m) * (bit + 1) for m, bit in zip(marks, bits)]
        a = [
            marks[0] * bits[0] + (1 - marks[0]) * high,
            marks[1] * bits[1] + marks[0] * high + marks[2] * low,
            marks[2] * bits[2] + (1 - marks[2]) * low,
        ]
        return b, a
    if kind == 2:
        b = [(1 - m) * 3 * bit + m * (bit + 1) for m, bit in zip(marks, bits)]
        a = [m * t + (1 - m) * bit for m, bit in zip(marks, bits)]
        return b, a
    return [3 * bit for bit in bits], bits


def pair_class(kind, c, near_ref, ext, ext_off, acc, pick, rows8, spreads, tiles):
    count = 8 // 2**kind
    for leaf in range(8):
        b, _ = place(kind, c, leaf, 0)
        rows8[8 * leaf : 8 * leaf + 3, :] = ext_off[b[0], b[1], b[2]].astype(F32)
    spread = lax.dot_general(
        rows8[...].astype(BF16),
        pick[...],
        (((0,), (0,)), ((), ())),
        preferred_element_type=F32,
    )
    for n in range(24):
        spreads[n // 3, n % 3] = spread[:, n * NODES : (n + 1) * NODES]

    def step(n, carry):
        for u in range(UNROLL):
            leaf = (n * UNROLL + u) // count
            b, a = place(kind, c, leaf, (n * UNROLL + u) % count)
            d = [b[k] - 1 - a[k] for k in range(3)]
            own = ext_off[a[0] + 1, a[1] + 1, a[2] + 1].astype(F32)
            rows = [own[p : p + 1, :] - d[p].astype(F32) for p in range(3)]
            tile(rows, spreads.at[leaf], tiles.at[u])
            index = 9 * (d[0] + 1) + 3 * (d[1] + 1) + d[2] + 1
            mask = near_ref[a[0], a[1], a[2], index].astype(F32)
            sampled = ext[b[0], b[1], b[2]] * mask.astype(BF16)
            acc[a[0], a[1], a[2]] -= jnp.dot(
                sampled, tiles[u], preferred_element_type=F32
            )
        return carry

    lax.fori_loop(0, 8 * count // UNROLL, step, 0)


def prepare(pick, rows8):
    row = lax.broadcasted_iota(jnp.int32, pick.shape, 0)
    lane = lax.broadcasted_iota(jnp.int32, pick.shape, 1)
    wanted = jnp.logical_and(row % 8 < 3, row // 8 * 3 + row % 8 == lane // NODES)
    pick[...] = wanted.astype(F32).astype(BF16)
    rows8[...] = jnp.zeros_like(rows8)


def all_pairs(arrive, *refs):
    arrive(0, 0)
    pair_class(0, 0, *refs)
    for kind in (1, 2):

        def step(c, carry):
            arrive(kind, c)
            pair_class(kind, c, *refs)
            return carry

        lax.fori_loop(0, 3, step, 0)
    arrive(3, 0)
    pair_class(3, 0, *refs)


def kind_of(d):
    size = sum(abs(s) for s in d)
    if size == 3:
        return 3, 0
    return size, [abs(s) for s in d].index(1 if size == 1 else 0)


def near_kernel(
    sizes,
    near_ref,
    sketch,
    test,
    offs,
    far,
    grams,
    box,
    group,
    ext,
    ext_off,
    pick,
    rows8,
    spreads,
    tiles,
    stage,
    slots,
    sends,
    recvs,
    o_sends,
    o_recvs,
    g_sends,
    g_recvs,
    fetch_sem,
):
    names = ("gx", "gy", "gz")
    me = [lax.axis_index(n) for n in names]

    def inside(d):
        ok = None
        for k in range(3):
            if d[k] != 0:
                here = (me[k] < sizes[k] - 1) if d[k] == 1 else (me[k] > 0)
                ok = here if ok is None else jnp.logical_and(ok, here)
        return ok

    def copies(d):
        n = directions().index(d)
        to = tuple(me[k] + d[k] for k in range(3))
        s, t = source_window(d), landing_window(d)
        return (
            pltpu.make_async_remote_copy(
                src_ref=offs.at[s[0], s[1], s[2]],
                dst_ref=ext_off.at[t[0], t[1], t[2]],
                send_sem=o_sends.at[n],
                recv_sem=o_recvs.at[n],
                device_id=to,
                device_id_type=MESH,
            ),
            pltpu.make_async_remote_copy(
                src_ref=test.at[s[0], s[1], s[2]],
                dst_ref=ext.at[t[0], t[1], t[2]],
                send_sem=sends.at[n],
                recv_sem=recvs.at[n],
                device_id=to,
                device_id_type=MESH,
            ),
        )

    fetch = pltpu.make_async_copy(sketch, far, fetch_sem)
    fetch.start()
    barrier = pltpu.get_barrier_semaphore()
    for d in directions():

        @pl.when(inside(d))
        def _():
            to = tuple(me[k] + d[k] for k in range(3))
            pl.semaphore_signal(barrier, inc=1, device_id=to, device_id_type=MESH)

    spans = [
        1 + (me[k] > 0).astype(jnp.int32) + (me[k] < sizes[k] - 1).astype(jnp.int32)
        for k in range(3)
    ]
    for k in range(3):
        for side in (0, 1):
            at = [slice(None)] * 3
            at[k] = slice(3 * side, 3 * side + 1)

            @pl.when(me[k] == side * (sizes[k] - 1))
            def _():
                ext[at[0], at[1], at[2]] = jnp.zeros_like(ext[at[0], at[1], at[2]])
                ext_off[at[0], at[1], at[2]] = jnp.zeros_like(ext_off[at[0], at[1], at[2]])

    pl.semaphore_wait(barrier, spans[0] * spans[1] * spans[2] - 1)
    order = sorted(directions(), key=kind_of)
    for d in order:

        @pl.when(inside(d))
        def _():
            for c in copies(d):
                c.start()

    prepare(pick, rows8)
    ext[1:3, 1:3, 1:3] = test[...]
    ext_off[1:3, 1:3, 1:3] = offs[...]
    fetch.wait()

    def arrive(kind, c):
        for d in order:
            if kind_of(d)[0] == kind:

                @pl.when(jnp.logical_and(c == kind_of(d)[1], inside([-s for s in d])))
                def _():
                    for copy in copies(d):
                        copy.wait_recv()

    all_pairs(arrive, near_ref, ext, ext_off, far, pick, rows8, spreads, tiles)
    leaf_grams(far, grams, box, stage)
    swaps = group_copies(me, box, slots, g_sends, g_recvs)
    for c in swaps:
        c.start()
    collect(me, swaps, box, slots, group)
    for d in order:

        @pl.when(inside(d))
        def _():
            for c in copies(d):
                c.wait_send()


def near_field(mesh, sketch, test, offs, near):
    sizes = tuple(mesh.shape[n] for n in ("gx", "gy", "gz"))
    vmem = pl.BlockSpec(memory_space=pltpu.VMEM)
    return pl.pallas_call(
        functools.partial(near_kernel, sizes),
        out_shape=[
            jax.ShapeDtypeStruct(s, F32)
            for s in (sketch.shape, (8, RANK, 2 * RANK), (RANK, 2 * RANK), (RANK, 2 * RANK))
        ],
        in_specs=[
            pl.BlockSpec(memory_space=pltpu.SMEM),
            pl.BlockSpec(memory_space=pl.ANY),
            vmem,
            vmem,
        ],
        out_specs=[vmem] * 4,
        scratch_shapes=[
            pltpu.VMEM((4, 4, 4) + test.shape[3:], BF16),
            pltpu.VMEM((4, 4, 4) + offs.shape[3:], BF16),
            pltpu.VMEM((64, 24 * NODES), BF16),
            pltpu.VMEM((64, NODES), F32),
            pltpu.VMEM((8, 3, NODES, NODES), F32),
            pltpu.VMEM((UNROLL, 3 * NODES, 3 * NODES), BF16),
            pltpu.VMEM((2 * RANK, 3 * NODES), F32),
            pltpu.VMEM((8, RANK, 2 * RANK), F32),
            pltpu.SemaphoreType.DMA((26,)),
            pltpu.SemaphoreType.DMA((26,)),
            pltpu.SemaphoreType.DMA((26,)),
            pltpu.SemaphoreType.DMA((26,)),
            pltpu.SemaphoreType.DMA((7,)),
            pltpu.SemaphoreType.DMA((7,)),
            pltpu.SemaphoreType.DMA,
        ],
        compiler_params=pltpu.CompilerParams(
            collective_id=0, has_side_effects=True, vmem_limit_bytes=48 << 20
        ),
    )(near, sketch, test, offs)


def gram(rows, stage):
    stage[RANK:, :] = rows
    return lax.dot_general(
        rows,
        stage[...],
        (((1,), (1,)), ((), ())),
        precision=HIGHEST,
        preferred_element_type=F32,
    )


def product(left, right):
    return jnp.dot(left, right, precision=HIGHEST, preferred_element_type=F32)


def halves(x):
    high = x.astype(BF16)
    return high, (x - high.astype(F32)).astype(BF16)


def rows_product(left, right):
    left = jnp.concatenate(halves(left), axis=0)
    right = jnp.concatenate(halves(right), axis=0)
    parts = lax.dot_general(
        left, right, (((1,), (1,)), ((), ())), preferred_element_type=F32
    )
    half = parts[:RANK] + parts[RANK:]
    return half + pltpu.roll(half, RANK, axis=1)


def gram_near_identity(rows):
    return rows_product(rows, rows)


def near_product(left, right):
    lefts, (high, low) = halves(left), halves(right)
    parts = jnp.dot(jnp.concatenate(lefts, axis=0), high, preferred_element_type=F32)
    rest = jnp.dot(lefts[0], low, preferred_element_type=F32)
    return parts[:RANK] + (parts[RANK:] + rest)


def with_eye(matrix):
    row = lax.broadcasted_iota(jnp.int32, (RANK, 2 * RANK), 0)
    lane = lax.broadcasted_iota(jnp.int32, (RANK, 2 * RANK), 1)
    return jnp.where(lane < RANK, (row == lane).astype(F32), matrix)


def put(state, slot, matrix, stride=8):
    state[pl.ds(slot, RANK, stride=stride), :] = with_eye(matrix)


def inverse_of(state, slot, stride=8):
    return state[pl.ds(slot, RANK, stride=stride), :][:, :RANK]


def splat(row, lane):
    return jnp.broadcast_to(row[:, RANK + lane : RANK + lane + 1], row.shape)


def eliminate(rows, start):
    c = {
        (k, m): splat(rows[k], start + m) for k in range(BLOCK) for m in range(k, BLOCK)
    }
    for k in range(BLOCK):
        inverse = lax.rsqrt(c[k, k])
        f = {m: c[k, m] * inverse for m in range(k + 1, BLOCK)}
        for m in range(k + 1, BLOCK):
            for n in range(m, BLOCK):
                c[m, n] = c[m, n] - f[m] * f[n]
        rows[k] = rows[k] * inverse
        for m in range(k + 1, BLOCK):
            rows[m] = rows[m] - f[m] * rows[k]


def factor(state, top):
    sublane = lax.broadcasted_iota(jnp.int32, (8, 2 * RANK), 0)
    for start in range(0, RANK, BLOCK):
        rows = [state[8 * (start + k) : 8 * (start + k) + 8, :] for k in range(BLOCK)]
        eliminate(rows, start)
        for k in range(BLOCK):
            state[8 * (start + k) : 8 * (start + k) + 8, :] = rows[k]
        for i in range(start + BLOCK, RANK):
            row = state[8 * i : 8 * i + 8, :]
            for k in range(BLOCK):
                row = row - splat(rows[k], i) * rows[k]
            state[8 * i : 8 * i + 8, :] = row
        at = [slice(2 * (start + k), 2 * (start + k) + 2) for k in range(BLOCK)]
        rows = [jnp.concatenate([top[at[k], :]] * 4, axis=0) for k in range(BLOCK)]
        eliminate(rows, start)
        turned = []
        for k in range(BLOCK):
            top[at[k], :] = rows[k][:2]
            turn = rows[k]
            for t in range(1, 4):
                turn = jnp.where(
                    sublane // 2 == t, pltpu.roll(rows[k], 2 * RANK - t, axis=1), turn
                )
            turned.append(turn)
        for i in range(start + BLOCK, RANK, 4):
            four = top[2 * i : 2 * i + 8, :]
            for k in range(BLOCK):
                four = four - splat(turned[k], i) * rows[k]
            top[2 * i : 2 * i + 8, :] = four


def leaves():
    return [(i, j, k) for i in range(2) for j in range(2) for k in range(2)]


def leaf_grams(far, grams, box, stage):
    stage[:RANK, :] = jnp.zeros((RANK, stage.shape[1]), F32)
    total = None
    for n, a in enumerate(leaves()):
        g = gram(far[a], stage)
        grams[n] = g
        total = g if total is None else total + g
    box[...] = total


def first_kernel(grams, box, group, leaf_state, top_state):
    for n in range(8):
        put(leaf_state, n, grams[n])
    put(top_state, 0, box[...], 2)
    put(top_state, 1, group[...], 2)
    factor(leaf_state, top_state)


def apply_kernel(
    far, leaf_state, top_state, q1, w, v, grams2, box2, group2, own2, slots, sends, recvs
):
    me = [lax.axis_index(n) for n in ("gx", "gy", "gz")]
    barrier = pltpu.get_barrier_semaphore()
    for to in partners(me)[1]:
        pl.semaphore_signal(barrier, inc=1, device_id=to, device_id_type=MESH)
    group_inverse = inverse_of(top_state, 1, 2)
    total = None
    for n, a in enumerate(leaves()):
        x = product(group_inverse, far[a])
        v[n] = x
        g = gram_near_identity(x)
        total = g if total is None else total + g
    own2[...] = total
    pl.semaphore_wait(barrier, 7)
    copies = group_copies(me, own2, slots, sends, recvs)
    for c in copies:
        c.start()
    box_inverse = inverse_of(top_state, 0, 2)
    total = None
    for n, a in enumerate(leaves()):
        both = jnp.concatenate([inverse_of(leaf_state, n), box_inverse], axis=0)
        x = product(both, far[a])
        q1[n] = x[:RANK]
        w[n] = x[RANK:]
        grams2[n] = gram_near_identity(x[:RANK])
        g = gram_near_identity(x[RANK:])
        total = g if total is None else total + g
    box2[...] = total
    collect(me, copies, own2, slots, group2)


def second_kernel(q1, w, v, grams2, box2, group2, leaf_out, level_out, nested_out, leaf_state, top_state):
    for n in range(8):
        put(leaf_state, n, grams2[n])
    put(top_state, 0, box2[...], 2)
    put(top_state, 1, group2[...], 2)
    factor(leaf_state, top_state)
    width = q1.shape[2]
    box_inverse = inverse_of(top_state, 0, 2) * math.sqrt(8 * RANK)
    group_inverse = inverse_of(top_state, 1, 2) * (8.0 * math.sqrt(width))
    left_lanes = lax.broadcasted_iota(jnp.int32, (RANK, 2 * RANK), 1) < RANK
    for pair in range(4):
        blocks = []
        for n in (2 * pair, 2 * pair + 1):
            a = leaves()[n]
            x = near_product(inverse_of(leaf_state, n), q1[n])
            leaf_out[a] = x * math.sqrt(width)
            nested_out[a] = near_product(group_inverse, v[n])
            blocks.append(rows_product(near_product(box_inverse, w[n]), x))
        level_out[0, 0, 0, :, 2 * RANK * pair : 2 * RANK * (pair + 1)] = jnp.where(
            left_lanes, blocks[0], blocks[1]
        )


def partners(me):
    bits = [m % 2 for m in me]
    others = []
    for n in range(1, 8):
        flip = (n // 4, n // 2 % 2, n % 2)
        others.append(tuple(me[k] + flip[k] * (1 - 2 * bits[k]) for k in range(3)))
    return (bits[0] * 2 + bits[1]) * 2 + bits[2], others


def group_copies(me, own, slots, sends, recvs):
    here, others = partners(me)
    return [
        pltpu.make_async_remote_copy(
            src_ref=own,
            dst_ref=slots.at[here],
            send_sem=sends.at[n],
            recv_sem=recvs.at[n],
            device_id=to,
            device_id_type=MESH,
        )
        for n, to in enumerate(others)
    ]


def collect(me, copies, own, slots, total):
    slots[partners(me)[0]] = own[...]
    for c in copies:
        c.wait_recv()
    value = slots[0]
    for n in range(1, 8):
        value = value + slots[n]
    total[...] = value
    for c in copies:
        c.wait_send()


VMEM = pl.BlockSpec(memory_space=pltpu.VMEM)


def local(kernel, outs, scratch, *args):
    return pl.pallas_call(
        kernel,
        out_shape=[jax.ShapeDtypeStruct(s, F32) for s in outs],
        in_specs=[VMEM] * len(args),
        out_specs=[VMEM] * len(outs),
        scratch_shapes=[pltpu.VMEM(s, F32) for s in scratch],
        compiler_params=pltpu.CompilerParams(vmem_limit_bytes=48 << 20),
    )(*args)


def finish(far, grams, box, group):
    width = far.shape[4]
    square, slab = (RANK, 2 * RANK), (8, RANK, width)
    state = (8 * RANK, 2 * RANK)
    states = local(first_kernel, [state, (2 * RANK, 2 * RANK)], [], grams, box, group)
    outs = [slab, slab, slab, (8,) + square, square, square]
    applied = pl.pallas_call(
        apply_kernel,
        out_shape=[jax.ShapeDtypeStruct(s, F32) for s in outs],
        in_specs=[VMEM] * 3,
        out_specs=[VMEM] * 6,
        scratch_shapes=[
            pltpu.VMEM(square, F32),
            pltpu.VMEM((8,) + square, F32),
            pltpu.SemaphoreType.DMA((7,)),
            pltpu.SemaphoreType.DMA((7,)),
        ],
        compiler_params=pltpu.CompilerParams(
            collective_id=1, has_side_effects=True, vmem_limit_bytes=48 << 20
        ),
    )(far, *states)
    return local(
        second_kernel,
        [far.shape, (1, 1, 1, RANK, 8 * RANK), far.shape],
        [state, (2 * RANK, 2 * RANK)],
        *applied,
    )


def solution(mesh):
    placed = (
        P("gx", "gy", "gz", None, None),
        P("gx", "gy", "gz", None, None),
        P("gx", "gy", "gz", None, None),
        P("gx", "gy", "gz", None),
    )

    def body(sketch, test_matrix, offsets, near):
        near_results = near_field(mesh, sketch, test_matrix, offsets, near)
        return tuple(finish(*near_results))

    return jax.shard_map(
        body,
        mesh=mesh,
        in_specs=placed,
        out_specs=placed[:3],
        check_vma=False,
    )
```
